32 devices in a mesh: gx: 2 (over x), gy: 4 (over z), gz: 4 (over y, core).
Axes of the slice: x: 2, y: 2, z: 4, core: 2. Of those that a mesh axis runs over, the one named last changes fastest.
Arguments:
- local_displacement: float32 [2, 4, 4, 6, 128, 128], P('gx', 'gy', 'gz'), may hold values from -6 to 6
- coarse_load: float32 [2, 4, 4, 6, 128], P('gx', 'gy', 'gz'), may hold values from -12 to 12
- flexibility: float32 [2, 4, 4, 768, 768], P('gx', 'gy', 'gz'), as said below
- block_map: int32 [2, 4, 4, 768], P('gx', 'gy', 'gz'), may hold values from 0 to 767, each once within a row
- mode_counts: int32 [2, 4, 4], P('gx', 'gy', 'gz'), may hold values from 3 to 6, as said below
- mode_traces: float32 [2, 4, 4, 6, 6, 128], P('gx', 'gy', 'gz')
- coarse_rows: float32 [2, 4, 4, 6, 192], P('gx', 'gy', 'gz'), as said below
- stored_dirs: float32 [2, 4, 4, 40, 6, 128], P('gx', 'gy', 'gz'), as said below
- stored_images: float32 [2, 4, 4, 40, 6, 128], P('gx', 'gy', 'gz'), as said below
- stored_curv: float32 [40], replicated, may hold values from 1 to 4
Outputs:
- multipliers: float32 [2, 4, 4, 6, 128, 128], P('gx', 'gy', 'gz')
- residual: float32 [2, 4, 4, 6, 128, 128], P('gx', 'gy', 'gz')
The draws below stay inside these ranges and needn't reach their ends.
Inputs may be any that keep to these rules, and one draw needn't show every extreme that they name: `flexibility`: each subdomain's matrix is symmetric positive definite. `coarse_rows`: read as a [192, 192] matrix it is exactly symmetric: the inverse of G^T G for the coarse basis G of the present modes, with ones added on the diagonal of absent modes. `mode_counts`: modes numbered from the count on are absent. `block_map`: each subdomain's row names every interface position once. `stored_dirs`: both copies of every face agree: slot 2a of a subdomain equals slot 2a+1 of its lower neighbour along grid dimension a. `stored_images`: both copies of every face agree: slot 2a of a subdomain equals slot 2a+1 of its lower neighbour along grid dimension a.
All inputs are finite; a program needn't handle non-finite values.
Results may differ from the reference program's by a relative error of at most 0.0003.
Values sent between devices are 32-bit elements; how exact they have to be, the bound alone decides.
No kernel may reach another device: no remote copies, remote signals or barrier semaphores. Data moves between devices by JAX's collectives and lax.ppermute only.
A program may use at most 128 MiB of HBM per device.

```python
import math
import jax
import jax.numpy as jnp
from jax import lax

FACE = 128
RHS = 128
STORED = 40
RM = 6
ITERS = 3
NB = 768
SX = 2
SY = 4
SZ = 4
SUBS = 32
CMODES = 192


def face_draw(draw_key, shape):
    return jax.random.normal(draw_key, shape, jnp.float32)


def coarse_bundle(key):
    counts = jax.random.randint(jax.random.fold_in(key, 101), (SX, SY, SZ), 3, RM + 1, dtype=jnp.int32)
    shared = face_draw(jax.random.fold_in(key, 102), (SX, SY, SZ, RM, 3, FACE))
    own_part = face_draw(jax.random.fold_in(key, 103), (SX, SY, SZ, RM, 6, FACE))
    slots = []
    for grid_dim in range(3):
        plus_face = shared[:, :, :, :, grid_dim]
        slots.append(jnp.roll(plus_face, 1, axis=grid_dim))
        slots.append(plus_face)
    traces = (jnp.stack(slots, axis=4) + 0.25 * own_part) * FACE ** (-0.5)
    present = (jnp.arange(RM, dtype=jnp.int32)[None, None, None, :] < counts[..., None]).astype(jnp.float32)
    masked = traces * present[..., None, None]
    diagonal_blocks = jnp.einsum('xyzmsf,xyznsf->xyzmn', masked, masked).reshape(SUBS, RM, RM)
    unit = jnp.eye(SUBS, dtype=jnp.float32)
    gram = jnp.einsum('st,smn->smtn', unit, diagonal_blocks)
    for grid_dim in range(3):
        above = jnp.roll(masked[:, :, :, :, 2 * grid_dim], -1, axis=grid_dim)
        coupling = -jnp.einsum('xyzmf,xyznf->xyzmn', masked[:, :, :, :, 2 * grid_dim + 1], above).reshape(SUBS, RM, RM)
        shifter = jnp.roll(unit.reshape(SX, SY, SZ, SUBS), -1, axis=grid_dim).reshape(SUBS, SUBS)
        gram = gram + jnp.einsum('st,smn->smtn', shifter, coupling) + jnp.einsum('st,smn->tnsm', shifter, coupling)
    absent = (1.0 - present).reshape(CMODES)
    matrix = gram.reshape(CMODES, CMODES) + jnp.diag(absent)
    inverse = jnp.linalg.inv(matrix)
    inverse = 0.5 * (inverse + inverse.T)
    return (counts, traces, inverse.reshape(SX, SY, SZ, RM, CMODES))


def draw_mode_counts(key, part):
    return coarse_bundle(key)[0]


def draw_mode_traces(key, part):
    return coarse_bundle(key)[1]


def draw_coarse_rows(key, part):
    return coarse_bundle(key)[2]


def stored_slabs(key, salt, spread):
    raw_key = jax.random.fold_in(key, salt)
    owned = jax.random.normal(raw_key, (SX, SY, SZ, STORED, 3, FACE), jnp.float32) * spread
    slots = []
    for grid_dim in range(3):
        plus_face = owned[:, :, :, :, grid_dim]
        slots.append(jnp.roll(plus_face, 1, axis=grid_dim))
        slots.append(plus_face)
    return jnp.stack(slots, axis=4)


def draw_stored_dirs(key, part):
    return stored_slabs(key, 201, 0.1)


def draw_stored_images(key, part):
    return stored_slabs(key, 202, (3.0 * FACE * SUBS) ** (-0.5))


def draw_flexibility(key, part):
    raw_key = jax.random.fold_in(key, 301)
    raw = jax.random.normal(raw_key, (SX, SY, SZ, NB, NB), jnp.float32)
    symmetric = (raw + jnp.swapaxes(raw, -1, -2)) * (0.35 / (2.0 * NB) ** 0.5)
    scales = jnp.exp(jax.random.uniform(jax.random.fold_in(key, 302), (SX, SY, SZ, NB), jnp.float32, jnp.log(0.7), jnp.log(1.4)))
    core = symmetric + jnp.eye(NB, dtype=jnp.float32)
    return core * (scales[..., :, None] * scales[..., None, :])


def block_levels(own_key, dims, pieces, low, high):
    gain, own = 1.0, jax.random.fold_in(own_key, 6)
    for dim, parts in pieces:
        draws = jnp.exp(jax.random.uniform(jax.random.fold_in(own, dim), (parts,), jnp.float32, low / len(pieces), high / len(pieces)))
        gain = gain * jnp.repeat(draws, dims[dim] // parts).reshape([-1 if axis == dim else 1 for axis in range(len(dims))])
    return gain


def normal_values(rng, extent, scale, most, shards=(), held_as=jnp.bfloat16):
    values = jax.random.normal(rng, extent, jnp.float32) * scale
    if len(shards) > 0:
        values = block_levels(rng, extent, shards, -0.22, 0.18) * values
    return jnp.clip(values, min=-most, max=most).astype(held_as)


def setup_inputs(seed: int = 0) -> dict:
    key_list = jax.random.split(jax.random.key(seed), 11)
    local_displacement = normal_values(key_list[0], (SX, SY, SZ, 6, FACE, RHS), 1.0, 6.0, ((0, 2), (1, 4), (2, 4)), jnp.float32)
    coarse_load = normal_values(key_list[1], (SX, SY, SZ, RM, RHS), 2.0, 12.0, ((0, 2), (1, 4), (2, 4)), jnp.float32)
    flexibility = draw_flexibility(jax.random.fold_in(key_list[10], 71), 0)
    block_map = jax.vmap(lambda own: jax.random.permutation(own, NB))(jax.random.split(key_list[3], SX * SY * SZ)).reshape((SX, SY, SZ, NB)).astype(jnp.int32)
    mode_counts = draw_mode_counts(jax.random.fold_in(key_list[10], 71), 0)
    mode_traces = draw_mode_traces(jax.random.fold_in(key_list[10], 71), 0)
    coarse_rows = draw_coarse_rows(jax.random.fold_in(key_list[10], 71), 0)
    stored_dirs = draw_stored_dirs(jax.random.fold_in(key_list[10], 71), 0)
    stored_images = draw_stored_images(jax.random.fold_in(key_list[10], 71), 0)
    stored_curv = jnp.clip(jnp.exp(jax.random.uniform(key_list[9], (STORED,), jnp.float32, math.log(1.0), math.log(4.0))), 1.0, 4.0)
    return {"local_displacement": local_displacement, "coarse_load": coarse_load, "flexibility": flexibility, "block_map": block_map, "mode_counts": mode_counts, "mode_traces": mode_traces, "coarse_rows": coarse_rows, "stored_dirs": stored_dirs, "stored_images": stored_images, "stored_curv": stored_curv}


precise = lax.Precision.HIGHEST

def assemble(field):
    slots = []
    for grid_dim in range(3):
        minus_side = field[:, :, :, 2 * grid_dim]
        plus_side = field[:, :, :, 2 * grid_dim + 1]
        slots.append(minus_side + jnp.roll(plus_side, 1, axis=grid_dim))
        slots.append(plus_side + jnp.roll(minus_side, -1, axis=grid_dim))
    return jnp.stack(slots, axis=3)

def single_apply(matrix, mapping, vector):
    picked = vector[mapping]
    product = jnp.dot(matrix, picked, precision=precise)
    return jnp.zeros_like(vector).at[mapping].set(product)

def flex_apply(flexibility, block_map, field):
    flat = field.reshape(SUBS, NB, RHS)
    result = jax.vmap(single_apply)(flexibility.reshape(SUBS, NB, NB), block_map.reshape(SUBS, NB), flat)
    return result.reshape(field.shape)

def coarse_solve(coarse_rows, loads):
    matrix = coarse_rows.reshape(CMODES, CMODES)
    return jnp.dot(matrix, loads.reshape(CMODES, RHS), precision=precise).reshape(SX, SY, SZ, RM, RHS)

def graph(signed, alpha):
    return assemble(jnp.einsum('xyzmsf,xyzmr->xyzsfr', signed, alpha, precision=precise))

def inner(first, second):
    return jnp.sum(first[:, :, :, 1::2] * second[:, :, :, 1::2], axis=(0, 1, 2, 3, 4))

def reference(local_displacement, coarse_load, flexibility, block_map, mode_counts, mode_traces, coarse_rows, stored_dirs, stored_images, stored_curv):
    signs = jnp.array([-1.0, 1.0, -1.0, 1.0, -1.0, 1.0], jnp.float32)
    field_signs = signs[:, None, None]
    present = (jnp.arange(RM, dtype=jnp.int32)[None, None, None, :] < mode_counts[..., None]).astype(jnp.float32)
    signed = mode_traces * present[..., None, None] * signs[:, None]

    def project(field):
        partial_loads = jnp.einsum('xyzmsf,xyzsfr->xyzmr', signed, field, precision=precise)
        return field - graph(signed, coarse_solve(coarse_rows, partial_loads))
    lam = graph(signed, coarse_solve(coarse_rows, coarse_load))
    moved = flex_apply(flexibility, block_map, field_signs * lam)
    resid = project(assemble(field_signs * (local_displacement - moved)))
    directions, images, curves = ([], [], [])
    for step in range(ITERS):
        stored_part = jnp.einsum('xyzisf,xyzsfr->ir', stored_images[:, :, :, :, 1::2], resid[:, :, :, 1::2], precision=precise)
        beta = stored_part / stored_curv[:, None]
        gammas = [inner(images[index], resid) / curves[index] for index in range(len(images))]
        direction = resid - jnp.einsum('xyzisf,ir->xyzsfr', stored_dirs, beta, precision=precise)
        for index in range(len(directions)):
            direction = direction - directions[index] * gammas[index]
        image_now = project(assemble(field_signs * flex_apply(flexibility, block_map, field_signs * direction)))
        curve = inner(direction, image_now)
        rate = inner(direction, resid) / curve
        lam = lam + rate * direction
        resid = resid - rate * image_now
        directions.append(direction)
        images.append(image_now)
        curves.append(curve)
    return (lam, resid)
```

```python
import jax
import jax.numpy as jnp
from jax import lax
from jax.sharding import PartitionSpec as P

ITERS = 3
AXES = ("gx", "gy", "gz")

precise = lax.Precision.HIGHEST


def mm(a, b):
    return jnp.dot(a, b, precision=precise)


def padded(x, rows):
    return jnp.pad(x, ((0, rows - x.shape[0]),) + ((0, 0),) * (x.ndim - 1))


def shift(x, axis, step):
    n = lax.axis_size(axis)
    return lax.ppermute(x, axis, [(i, (i + step) % n) for i in range(n)])


def swap_faces(faces):
    out = []
    for a, axis in enumerate(AXES):
        lower, upper = faces[2 * a], faces[2 * a + 1]
        if lax.axis_size(axis) == 2:
            both = shift(jnp.stack([upper, lower]), axis, 1)
            out += [both[0], both[1]]
        else:
            out += [shift(upper, axis, 1), shift(lower, axis, -1)]
    return out


def exchange(gathered, summed):
    for axis in reversed(AXES):
        n = lax.axis_size(axis)
        if n & (n - 1):
            gathered = lax.all_gather(gathered, axis, axis=0, tiled=True)
            summed = None if summed is None else lax.psum(summed, axis)
            continue
        index = lax.axis_index(axis)
        for b in range(n.bit_length() - 1):
            pairs = [(i, i ^ (1 << b)) for i in range(n)]
            rows = gathered.shape[0]
            message = gathered if summed is None else jnp.concatenate([gathered, summed])
            got = lax.ppermute(message, axis, pairs)
            theirs = got[:rows]
            first = ((index >> b) & 1) == 0
            gathered = jnp.concatenate(
                [jnp.where(first, gathered, theirs), jnp.where(first, theirs, gathered)]
            )
            if summed is not None:
                summed = summed + got[rows:]
    return gathered, summed


def per_device(
    local_displacement,
    coarse_load,
    flexibility,
    block_map,
    mode_counts,
    mode_traces,
    coarse_rows,
    stored_dirs,
    stored_images,
    stored_curv,
):
    displacement = local_displacement[0, 0, 0]
    slots, face, rhs = displacement.shape
    size_nb = slots * face
    loads = coarse_load[0, 0, 0]
    flex = flexibility[0, 0, 0]
    mapping = block_map[0, 0, 0]
    rows = coarse_rows[0, 0, 0]
    nmodes = rows.shape[0]
    subs = rows.shape[1] // nmodes
    pm = -(-nmodes // 8) * 8
    stored = stored_curv.shape[0]
    sizes = [lax.axis_size(a) for a in AXES]
    here = [lax.axis_index(a) for a in AXES]

    def sub_index(pos):
        return (pos[0] * sizes[1] + pos[1]) * sizes[2] + pos[2]

    signs = jnp.where(jnp.arange(slots) % 2 == 0, -1.0, 1.0).astype(jnp.float32)
    odd = (jnp.arange(size_nb) // face) % 2 == 1
    present = (jnp.arange(nmodes, dtype=jnp.int32) < mode_counts[0, 0, 0]).astype(jnp.float32)
    signed = padded(mode_traces[0, 0, 0] * present[:, None, None] * signs[None, :, None], pm)
    modes = signed.reshape(pm, size_nb)
    images_t = stored_images[0, 0, 0].reshape(stored, size_nb)
    dirs_t = stored_dirs[0, 0, 0].reshape(stored, size_nb)
    reducer = jnp.concatenate([modes, jnp.where(odd[None, :], images_t, 0.0)])

    own_t = lax.dot_general(
        modes, jnp.concatenate([images_t, dirs_t]), (((1,), (1,)), ((), ())), precision=precise
    )
    own_c = jnp.pad(
        rows.reshape(nmodes, subs, nmodes), ((0, pm - nmodes), (0, 0), (0, pm - nmodes))
    ).reshape(pm, subs * pm)
    table, _ = exchange(jnp.concatenate([padded(loads, pm), own_c, own_t], axis=1), None)
    all_loads = table[:, :rhs]
    coarse = table[:, rhs : rhs + subs * pm]
    tangents = table[:, rhs + subs * pm :]
    others = swap_faces([signed[:, a] for a in range(slots)])

    pick = jnp.where(
        mapping[:, None] == jnp.arange(size_nb, dtype=jnp.int32)[None, :],
        jnp.repeat(signs, face)[None, :],
        0.0,
    ).astype(jnp.bfloat16)
    high = flex.astype(jnp.bfloat16)
    low = (flex - high.astype(jnp.float32)).astype(jnp.bfloat16)

    def renumber(x):
        left = lax.dot_general(
            pick, x, (((0,), (0,)), ((), ())), preferred_element_type=jnp.float32
        ).astype(jnp.bfloat16)
        return jnp.dot(left, pick, preferred_element_type=jnp.float32).astype(jnp.bfloat16)

    high, low = renumber(high), renumber(low)

    def operate(x):
        x_high = x.astype(jnp.bfloat16)
        x_low = (x - x_high.astype(jnp.float32)).astype(jnp.bfloat16)
        wide = jnp.dot(
            high, jnp.concatenate([x_high, x_low], axis=1), preferred_element_type=jnp.float32
        )
        return wide[:, :rhs] + wide[:, rhs:] + jnp.dot(low, x_high, preferred_element_type=jnp.float32)

    def assemble(x):
        parts = [x[a * face : (a + 1) * face] for a in range(slots)]
        return x + jnp.concatenate(swap_faces(parts))

    own_rows = lax.dynamic_slice_in_dim(coarse, sub_index(here) * pm, pm)
    near = []
    for a in range(3):
        for step in (-1, 1):
            pos = list(here)
            pos[a] = (pos[a] + step) % sizes[a]
            near.append(
                jnp.concatenate([own_rows, lax.dynamic_slice_in_dim(coarse, sub_index(pos) * pm, pm)])
            )
    both_modes = jnp.stack([jnp.concatenate([signed[:, a], others[a]]) for a in range(slots)])
    project = jnp.einsum("akf,akc->afc", both_modes, jnp.stack(near), precision=precise).reshape(
        size_nb, subs * pm
    )
    small = jnp.concatenate([mm(tangents.T, coarse), coarse])

    def inner(u, v):
        return jnp.sum(jnp.where(odd[:, None], u * v, 0.0), axis=0)

    lam = mm(project, all_loads)
    flat = displacement * signs[:, None, None]
    z = assemble(flat.reshape(size_nb, rhs) - operate(lam))
    local = mm(reducer, z)
    g, sums = exchange(local[:pm], local[pm:])
    reduced = mm(small[:stored], g)
    on_images = sums - reduced
    w = z - mm(project, g)
    directions, images, curves, coefs, on_w = [], [], [], [], []
    for step in range(ITERS):
        last = step == ITERS - 1
        beta = on_images / stored_curv[:, None]
        p = w - lax.dot_general(dirs_t, beta, (((0,), (0,)), ((), ())), precision=precise)
        for j in range(step):
            gamma = on_w[j] / curves[j]
            p = p - directions[j] * gamma
            beta = beta - coefs[j] * gamma
        z = assemble(operate(p))
        scalars = [inner(p, z), inner(p, w)]
        if not last:
            scalars += [inner(z, z), inner(z, w)] + [inner(q, z) for q in images]
        scalars = jnp.stack(scalars)
        scalars = padded(scalars, -(-scalars.shape[0] // 8) * 8)
        if last:
            g, sums = exchange(mm(modes, z), scalars)
            offset = 0
        else:
            local = mm(reducer, z)
            g, sums = exchange(local[:pm], jnp.concatenate([local[pm:], scalars]))
            offset = stored
        reduced = mm(small[: 2 * stored] if last else small, g)
        curve = sums[offset] + jnp.sum(beta * reduced[stored : 2 * stored], axis=0)
        rate = sums[offset + 1] / curve
        q = z - mm(project, g)
        lam = lam + rate * p
        if not last:
            on_images = on_images - rate * (sums[:stored] - reduced[:stored])
            norm = sums[offset + 2] - jnp.sum(g * reduced[2 * stored :], axis=0)
            on_w = [on_w[j] - rate * sums[offset + 4 + j] for j in range(step)]
            on_w.append(sums[offset + 3] - rate * norm)
        w = w - rate * q
        directions.append(p)
        images.append(q)
        curves.append(curve)
        coefs.append(beta)
    shape = (1, 1, 1, slots, face, rhs)
    return lam.reshape(shape), w.reshape(shape)


def solution(mesh):
    def spec(extra):
        return P("gx", "gy", "gz", *([None] * extra))

    return jax.shard_map(
        per_device,
        mesh=mesh,
        in_specs=(
            spec(3),
            spec(2),
            spec(2),
            spec(1),
            spec(0),
            spec(3),
            spec(2),
            spec(3),
            spec(3),
            P(),
        ),
        out_specs=(spec(3), spec(3)),
        check_vma=False,
    )
```
